32 devices in a mesh: gx: 4 (over z), gy: 2 (over y), gz: 4 (over x, core).
Axes of the slice: x: 2, y: 2, z: 4, core: 2. Of those that a mesh axis runs over, the one named last changes fastest.
Arguments:
- bodies: float32 [1920, 4, 128], P(('gx', 'gy', 'gz'))
- velocity: float32 [1920, 3, 128], P(('gx', 'gy', 'gz')), may hold values from -6 to 6
- select: int32 [32, 5, 16], P(('gx', 'gy', 'gz')), may hold values from 0 to 123, as said below
- pair_target: int32 [32, 1024], P(('gx', 'gy', 'gz')), may hold values from 0 to 59
- pair_source: int32 [32, 1024], P(('gx', 'gy', 'gz')), may hold values from 0 to 139
- counts: int32 [32], P(('gx', 'gy', 'gz')), may hold values from 256 to 1024, as said below
- departures: int32 [32, 12], P(('gx', 'gy', 'gz')), may hold values from 0 to 59, as said below
- owners: int32 [384, 1], P(('gx', 'gy', 'gz')), may hold values from 0 to 3; in each aligned block of 12 rows (0 to 11, 12 to 23, ...) at most 6 rows name the same one
Outputs:
- resident: float32 [1920, 7, 128], P(('gx', 'gy', 'gz'))
- moved_in: float32 [768, 7, 128], P(('gx', 'gy', 'gz'))
The draws below stay inside these ranges and needn't reach their ends.
Inputs may be any that keep to these rules, and one draw needn't show every extreme that they name: `select`: at step k every entry is below 60 + k * 16, and each list names the block 60 + k * 16 - 1. `counts`: some device has 1024 live pairs. `departures`: entries of one device are distinct. `owners`: no owner gets more than 6 blocks from one device, and that many in some devices.
All inputs are finite; a program needn't handle non-finite values.
Results may differ from the reference program's by a relative error of at most 0.0003.
Values sent between devices are 32-bit elements; how exact they have to be, the bound alone decides.
A program may use at most 64 MiB of HBM per device.

```python
import math
import jax
import jax.numpy as jnp
import numpy as np
from jax import lax

BS = 128
OWN = 60
SEND = 16
PMAX = 1024
NBITS = 5
POOL = 140
MOVE = 12
CAP = 6
N_GX = 4
N_GY = 2
N_GZ = 4
DEVICES = 32


def draw_bodies(key, part):
    subkeys = jax.random.split(jax.random.fold_in(key, 101), 2)
    places = jax.random.normal(subkeys[0], (DEVICES * OWN, 3, BS), jnp.float32)
    places = jnp.clip(places, -6.0, 6.0)
    masses = jnp.exp(jax.random.uniform(subkeys[1], (DEVICES * OWN, 1, BS), jnp.float32, jnp.log(0.05), jnp.log(0.5)))
    return jnp.concatenate([places, masses], axis=1).astype(jnp.float32)


def draw_select(key, part):
    subkeys = jax.random.split(jax.random.fold_in(key, 202), 2)
    steps_range = jnp.arange(NBITS, dtype=jnp.int32)
    ceiling = OWN + SEND * steps_range
    raw_draws = jax.random.randint(subkeys[0], (DEVICES, NBITS, SEND), 0, 1 << 30)
    picks = raw_draws % ceiling[None, :, None]
    forced_column = jax.random.randint(subkeys[1], (DEVICES, NBITS, 1), 0, SEND)
    columns = jnp.arange(SEND, dtype=jnp.int32)[None, None, :]
    return jnp.where(columns == forced_column, ceiling[None, :, None] - 1, picks).astype(jnp.int32)


def draw_counts(key, part):
    subkeys = jax.random.split(jax.random.fold_in(key, 303), 2)
    drawn = jax.random.randint(subkeys[0], (DEVICES,), PMAX // 4, PMAX + 1)
    busiest = jax.random.randint(subkeys[1], (), 0, DEVICES)
    return jnp.where(jnp.arange(DEVICES, dtype=jnp.int32) == busiest, PMAX, drawn).astype(jnp.int32)


def draw_departures(key, part):
    subkeys = jax.random.split(jax.random.fold_in(key, 404), DEVICES)
    shuffled = jax.vmap(lambda single: jax.random.permutation(single, OWN))(subkeys)
    return shuffled[:, :MOVE].astype(jnp.int32)


def place_ends(entries, stream_key, low, high):
    place = [jax.random.randint(jax.random.fold_in(stream_key, axis), (), 0, length) for axis, length in enumerate(entries.shape)]
    main_axis = entries.shape.index(max(entries.shape))
    beside = place[:main_axis] + [(place[main_axis] + 1) % entries.shape[main_axis]] + place[main_axis + 1:]
    return entries.at[tuple(place)].set(low).at[tuple(beside)].set(high)


def block_scale(own_key, shape, cuts, smallest, top_value):
    gain = 1.0
    for axis_at, shards_of in cuts:
        steps = jax.random.uniform(jax.random.fold_in(jax.random.fold_in(own_key, 6), axis_at), (shards_of,), jnp.float32, smallest / len(cuts), top_value / len(cuts))
        gain = gain * jnp.repeat(jnp.exp(steps), shape[axis_at] // shards_of).reshape((-1,) + (1,) * (len(shape) - 1 - axis_at))
    return gain


def deal_out(own_key, own, number, rows, amount, top, reach, lean):
    ranking = jax.random.permutation(own_key, amount)
    crowded, common = portions_of(amount, rows * top, reach, lean, True), portions_of(amount, rows * top, reach, lean, False)
    places = jnp.arange(amount)

    def named(lengths, rotation):
        used = int((lengths > 0).sum())
        fixed = max(1, used // 4)
        passed = fixed + (places - fixed + rotation * (used - fixed)) % max(1, amount - fixed)
        return jnp.zeros((amount,), jnp.int32).at[ranking[jnp.where(places < fixed, places, passed)]].set(jnp.asarray(lengths, jnp.int32))

    lengths = jnp.where(number % 4 == 0, named(crowded, number // 4), named(common, number - number // 4 - 1))
    mixed = jax.random.permutation(jax.random.fold_in(own, 3), amount)
    giver, taker = mixed[0:amount // 2 * 2:2], mixed[1:amount // 2 * 2:2]
    margin = jnp.minimum(lengths[giver] - 1, reach - lengths[taker]) // 2
    margin = jnp.where((giver == ranking[0]) | (taker == ranking[0]) | (lengths[taker] == 0), 0, jnp.maximum(margin, 0))
    passed = jax.random.randint(jax.random.fold_in(own, 4), (amount // 2,), 0, 1 << 20) % (margin + 1)
    lengths = lengths.at[giver].add(-passed).at[taker].add(passed)
    items = jnp.searchsorted(jnp.cumsum(lengths), jnp.arange(rows * top), side="right").astype(jnp.int32)
    table = items.reshape(top, rows).T
    table = table[jax.random.permutation(jax.random.fold_in(own, 1), rows)]
    rotation = jax.random.randint(jax.random.fold_in(own, 2), (rows, 1), 0, top)
    return jnp.take_along_axis(table, (jnp.arange(top)[None, :] + rotation) % top, axis=1)


def portions_of(number_of, total, limit, skew, full):
    loads = [(1 << 20) // math.isqrt(standing ** skew) + 1 for standing in range(1, number_of + 1)]
    largest = limit if full else min(limit, max(-(-total // number_of), total * loads[0] // sum(loads)))
    least = 1 if total - largest >= number_of - 1 else 0
    given, surplus = [largest] + [least] * (number_of - 1), total - largest - least * (number_of - 1)
    while surplus > 0:
        candidates = [i for i in range(1, number_of) if given[i] < largest] or [i for i in range(1, number_of) if given[i] < limit]
        whole, remaining = sum([loads[i] for i in candidates]), surplus
        for i in candidates:
            addition = min(limit - given[i], max(1, remaining * loads[i] // whole), surplus)
            given[i] = given[i] + addition
            surplus = surplus - addition
    return np.array(given)


def noise(key, shape, width, bound, cuts=(), held_as=jnp.bfloat16):
    factor_of = block_scale(key, shape, cuts, -0.22, 0.18) if cuts else 1.0
    result = jax.random.normal(key, shape, jnp.float32) * width * factor_of
    return jnp.minimum(jnp.maximum(result, -bound), bound).astype(held_as)


def setup_inputs(seed: int = 0) -> dict:
    streams_of = jax.random.split(jax.random.key(seed), 9)
    bodies = draw_bodies(jax.random.fold_in(streams_of[8], 71), 0)
    velocity = noise(streams_of[1], (DEVICES * OWN, 3, BS), 1.0, 6.0, ((0, 32),), jnp.float32)
    select = draw_select(jax.random.fold_in(streams_of[8], 71), 0)
    pair_target = place_ends(jax.random.randint(streams_of[3], (DEVICES, PMAX), 0, OWN), jax.random.fold_in(streams_of[3], 1), 0, OWN - 1).astype(jnp.int32)
    pair_source = place_ends(jax.random.randint(streams_of[4], (DEVICES, PMAX), 0, POOL), jax.random.fold_in(streams_of[4], 1), 0, POOL - 1).astype(jnp.int32)
    counts = draw_counts(jax.random.fold_in(streams_of[8], 71), 0)
    departures = draw_departures(jax.random.fold_in(streams_of[8], 71), 0)
    owners_keys = jax.random.split(jax.random.fold_in(streams_of[7], 1), (DEVICES * MOVE) // MOVE)
    owners_turns = jax.random.permutation(jax.random.fold_in(streams_of[7], 3), (DEVICES * MOVE) // MOVE)
    owners = jax.vmap(lambda own, number: deal_out(jax.random.fold_in(streams_of[7], 2), own, number, MOVE, N_GZ, 1, CAP, 1))(owners_keys, owners_turns).reshape((DEVICES * MOVE, 1))
    return dict(bodies=bodies, velocity=velocity, select=select, pair_target=pair_target, pair_source=pair_source, counts=counts, departures=departures, owners=owners)


soften = 0.01
timestep = 0.25
group_rows = 64

def block_forces(targets, sources, validity):
    delta_x = sources[:, 0, None, :] - targets[:, 0, :, None]
    offset_vertical = sources[:, 1, None, :] - targets[:, 1, :, None]
    delta_z = sources[:, 2, None, :] - targets[:, 2, :, None]
    radius_sq = delta_x * delta_x + offset_vertical * offset_vertical + delta_z * delta_z + soften
    weight = sources[:, 3, None, :] * lax.rsqrt(radius_sq) / radius_sq
    pull_sums = jnp.stack([lax.optimization_barrier(jnp.sum(delta_x * weight, axis=2)), lax.optimization_barrier(jnp.sum(offset_vertical * weight, axis=2)), lax.optimization_barrier(jnp.sum(delta_z * weight, axis=2))], axis=1)
    return pull_sums * validity[:, None, None]

def axis_bits(extent):
    return extent.bit_length() - 1

def reference(bodies, velocity, select, pair_target, pair_source, counts, departures, owners):
    bits_gx = axis_bits(N_GX)
    bits_gy = axis_bits(N_GY)
    bits_gz = axis_bits(N_GZ)
    every_device_list = jnp.arange(DEVICES, dtype=jnp.int32)
    anchor = every_device_list[:, None] * OWN + jnp.arange(OWN, dtype=jnp.int32)[None, :]
    flip_masks = [1 << bits_gz + bits_gy + bit_index for bit_index in range(bits_gx)]
    flip_masks = flip_masks + [1 << bits_gz + bit_index for bit_index in range(bits_gy)]
    flip_masks = flip_masks + [1 << bit_index for bit_index in range(bits_gz)]
    for step_index, flip_mask in enumerate(flip_masks):
        partner = jnp.bitwise_xor(every_device_list, flip_mask)
        picked = jnp.take_along_axis(anchor, select[:, step_index, :], axis=1)
        anchor = jnp.concatenate([anchor, picked[partner]], axis=1)
    source_ids = jnp.take_along_axis(anchor, pair_source, axis=1).astype(jnp.int32)
    target_ids = (every_device_list[:, None] * OWN + pair_target).astype(jnp.int32)
    in_range = (jnp.arange(PMAX, dtype=jnp.int32)[None, :] < counts[:, None]).astype(jnp.float32)
    members = jnp.arange(OWN, dtype=jnp.int32)
    groups = PMAX // group_rows

    def device_accel(pieces):
        target_rows, source_rows, validity, local_rows = pieces

        def add_group(running, group):
            target_group, source_group, valid_group, local_group = group
            pull_sums = block_forces(bodies[target_group], bodies[source_group], valid_group)
            onehot = (local_group[:, None] == members[None, :]).astype(jnp.float32)
            return (running + jnp.einsum('gk,gcb->kcb', onehot, pull_sums, precision=lax.Precision.HIGHEST), None)
        grouped = (target_rows.reshape(groups, group_rows), source_rows.reshape(groups, group_rows), validity.reshape(groups, group_rows), local_rows.reshape(groups, group_rows))
        total, _ = lax.scan(add_group, jnp.zeros((OWN, 3, BS), jnp.float32), grouped)
        return total
    accelerations = lax.map(device_accel, (target_ids, source_ids, in_range, pair_target))
    accelerations = accelerations.reshape(DEVICES * OWN, 3, BS)
    velocity_new = velocity + timestep * accelerations
    position = bodies[:, :3, :] + timestep * velocity_new
    refreshed_state = jnp.concatenate([position, bodies[:, 3:4, :], velocity_new], axis=1)
    updated_dev = refreshed_state.reshape(DEVICES, OWN, 7, BS)
    departed = jnp.any(members[None, :, None] == departures[:, None, :], axis=2)
    resident = jnp.where(departed[:, :, None, None], jnp.zeros_like(updated_dev), updated_dev).reshape(DEVICES * OWN, 7, BS)
    owner_rows = owners.reshape(DEVICES, MOVE)
    same_owner = owner_rows[:, :, None] == owner_rows[:, None, :]
    moves = jnp.arange(MOVE, dtype=jnp.int32)
    prior_positions = moves[None, :] < moves[:, None]
    place_slot_index = lax.optimization_barrier(jnp.sum((same_owner & prior_positions[None, :, :]).astype(jnp.int32), axis=2))
    body_routes_table = ((owner_rows[:, :, None, None] == jnp.arange(N_GZ, dtype=jnp.int32)[None, None, :, None]) & (place_slot_index[:, :, None, None] == jnp.arange(CAP, dtype=jnp.int32)[None, None, None, :])).astype(jnp.float32)
    leaving = updated_dev[every_device_list[:, None], departures]
    outbox = jnp.einsum('dmgc,dmrb->dgcrb', body_routes_table, leaving, precision=lax.Precision.HIGHEST)
    outbox = outbox.reshape(DEVICES // N_GZ, N_GZ, N_GZ, CAP, 7, BS)
    moved_in = jnp.swapaxes(outbox, 1, 2).reshape(DEVICES * N_GZ * CAP, 7, BS)
    return (resident, moved_in)
```

```python
import functools

import jax
import jax.numpy as jnp
from jax import lax
from jax.experimental import pallas as pl
from jax.experimental.pallas import tpu as pltpu
from jax.sharding import PartitionSpec as P

soften = 0.01
timestep = 0.25
unroll = 4


def swapped(value, axis, stride):
    mask = 2**stride
    pairs = [(source, source ^ mask) for source in range(lax.axis_size(axis))]
    return lax.ppermute(value, axis, pairs)


def spread(block):
    columns = jnp.concatenate([block, block], axis=0).T
    return [jnp.broadcast_to(columns[:, c : c + 1], (128, 128)) for c in range(4)]


def step_kernel(
    slot_total,
    target_ref,
    source_ref,
    count_ref,
    departures_ref,
    owners_ref,
    pool_ref,
    velocity_ref,
    resident_ref,
    outbox_ref,
    table,
    accel,
    used,
):
    pool_size = pool_ref.shape[0]
    own_blocks = velocity_ref.shape[0]
    span = pool_ref.shape[2]

    @pl.loop(0, pool_size)
    def _(b):
        for c, values in enumerate(spread(pool_ref[b])):
            table[b, c] = values

    accel[...] = jnp.zeros_like(accel)

    @pl.loop(0, (count_ref[0] + unroll - 1) // unroll)
    def _(group):
        for u in range(unroll):
            t = target_ref[group * unroll + u]
            s = source_ref[group * unroll + u]
            xt = jnp.broadcast_to(pool_ref[t, 0:1, :], (8, span))
            yt = jnp.broadcast_to(pool_ref[t, 1:2, :], (8, span))
            zt = jnp.broadcast_to(pool_ref[t, 2:3, :], (8, span))
            ax = ay = az = None
            for g in range(0, span, 8):
                dx = table[s, 0, g : g + 8, :] - xt
                dy = table[s, 1, g : g + 8, :] - yt
                dz = table[s, 2, g : g + 8, :] - zt
                inverse = lax.rsqrt(dx * dx + dy * dy + (dz * dz + soften))
                w = (table[s, 3, g : g + 8, :] * inverse) * (inverse * inverse)
                if ax is None:
                    ax, ay, az = dx * w, dy * w, dz * w
                else:
                    ax, ay, az = ax + dx * w, ay + dy * w, az + dz * w
            accel[t, 0] += ax
            accel[t, 1] += ay
            accel[t, 2] += az

    @pl.loop(0, own_blocks)
    def _(b):
        pull = jnp.sum(accel[b], axis=1)
        velocity_new = velocity_ref[b] + timestep * pull
        block = pool_ref[b]
        resident_ref[b, 0:3, :] = block[0:3] + timestep * velocity_new
        resident_ref[b, 3:4, :] = block[3:4]
        resident_ref[b, 4:7, :] = velocity_new

    outbox_ref[...] = jnp.zeros_like(outbox_ref)
    for g in range(used.shape[0]):
        used[g] = 0
    for m in range(departures_ref.shape[0]):
        d = departures_ref[m]
        owner = owners_ref[m]
        slot = used[owner]
        used[owner] = slot + 1
        outbox_ref[owner * slot_total + slot] = resident_ref[d]
        resident_ref[d] = jnp.zeros(resident_ref.shape[1:], jnp.float32)


def on_device(bodies, velocity, select, pair_target, pair_source, counts, departures, owners):
    own_blocks = bodies.shape[0]
    span = bodies.shape[2]
    pair_total = pair_target.shape[1]
    pool = bodies
    step = 0
    for axis in ("gx", "gy", "gz"):
        for bit in range(lax.axis_size(axis).bit_length() - 1):
            incoming = swapped(pool[select[0, step]], axis, bit)
            pool = jnp.concatenate([pool, incoming], axis=0)
            step += 1
    live = jnp.arange(pair_total, dtype=jnp.int32) < counts[0]
    targets = jnp.where(live, pair_target[0], own_blocks)
    sources = jnp.where(live, pair_source[0], 0)
    group_size = lax.axis_size("gz")
    move_count = departures.shape[1]
    slot_total = max(2, 2 * move_count // group_size)
    smem = pl.BlockSpec(memory_space=pltpu.SMEM)
    vmem = pl.BlockSpec(memory_space=pltpu.VMEM)
    resident, outbox = pl.pallas_call(
        functools.partial(step_kernel, slot_total),
        out_shape=(
            jax.ShapeDtypeStruct((own_blocks, 7, span), jnp.float32),
            jax.ShapeDtypeStruct((group_size * slot_total, 7, span), jnp.float32),
        ),
        in_specs=[smem] * 5 + [vmem] * 2,
        out_specs=(vmem, vmem),
        scratch_shapes=[
            pltpu.VMEM((pool.shape[0], 4, span, span), jnp.float32),
            pltpu.VMEM((own_blocks + 1, 3, 8, span), jnp.float32),
            pltpu.SMEM((group_size,), jnp.int32),
        ],
        compiler_params=pltpu.CompilerParams(vmem_limit_bytes=67043328),
        name="gravity",
    )(targets, sources, counts, departures[0], owners[:, 0], pool, velocity)
    arrived = lax.all_to_all(
        outbox.reshape(group_size, slot_total, 7, span), "gz", split_axis=0, concat_axis=0, tiled=True
    )
    return resident, arrived.reshape(group_size * slot_total, 7, span)


def solution(mesh):
    everywhere = ("gx", "gy", "gz")
    cube = P(everywhere, None, None)
    flat = P(everywhere, None)
    return jax.shard_map(
        on_device,
        mesh=mesh,
        in_specs=(cube, cube, cube, flat, flat, P(everywhere), flat, flat),
        out_specs=(cube, cube),
        check_vma=False,
    )
```

```python
import functools
import math

import jax
import jax.numpy as jnp
from jax import lax
from jax.experimental import pallas as pl
from jax.experimental.pallas import tpu as pltpu
from jax.sharding import PartitionSpec as P

soften = 0.01
timestep = 0.25
deepest_unroll = 16


def swapped(value, axis, stride):
    mask = 2**stride
    pairs = [(source, source ^ mask) for source in range(lax.axis_size(axis))]
    return lax.ppermute(value, axis, pairs)


def split(values):
    high = jnp.clip(values, -3.38e38, 3.38e38).astype(jnp.bfloat16).astype(jnp.float32)
    rest = values - high
    middle = rest.astype(jnp.bfloat16).astype(jnp.float32)
    return high, middle, rest - middle


def step_kernel(
    slot_total,
    target_ref,
    source_ref,
    count_ref,
    departures_ref,
    owners_ref,
    pool_ref,
    velocity_ref,
    resident_ref,
    outbox_ref,
    sources,
    targets,
    accel,
    used,
):
    pool_size = pool_ref.shape[0]
    own_blocks = velocity_ref.shape[0]
    span = pool_ref.shape[2]
    unroll = math.gcd(target_ref.shape[0], deepest_unroll)

    row = lax.broadcasted_iota(jnp.int32, (12, 4 * span), 0)
    lane = lax.broadcasted_iota(jnp.int32, (12, 4 * span), 1)
    picks = (row % 4 == lane // span).astype(jnp.float32)
    ones = (lax.broadcasted_iota(jnp.int32, (4, span), 0) < 3).astype(jnp.float32)

    @pl.loop(0, pool_size)
    def _(b):
        pieces = split(pool_ref[b])
        sources[b] = jnp.concatenate([*pieces, ones], axis=0).T.astype(jnp.bfloat16)

    @pl.loop(0, own_blocks + 1)
    def _(b):
        nothing = jnp.zeros((1, span), jnp.float32)
        rows = [
            jnp.concatenate([-piece[0:1], -piece[1:2], -piece[2:3], nothing], axis=1)
            for piece in split(pool_ref[b])
        ]
        rows.append(jnp.zeros((1, 4 * span), jnp.float32))
        targets[b] = jnp.concatenate([picks, *rows], axis=0).astype(jnp.bfloat16)

    accel[...] = jnp.zeros_like(accel)

    @pl.loop(0, (count_ref[0] + unroll - 1) // unroll)
    def _(group):
        for u in range(unroll):
            t = target_ref[group * unroll + u]
            s = source_ref[group * unroll + u]
            gaps = jnp.dot(sources[s], targets[t], preferred_element_type=jnp.float32)
            ax = ay = az = None
            for g in range(0, span, 8):
                dx = gaps[g : g + 8, 0:span]
                dy = gaps[g : g + 8, span : 2 * span]
                dz = gaps[g : g + 8, 2 * span : 3 * span]
                mass = gaps[g : g + 8, 3 * span :]
                inverse = lax.rsqrt(dx * dx + dy * dy + (dz * dz + soften))
                w = (mass * inverse) * (inverse * inverse)
                if ax is None:
                    ax, ay, az = dx * w, dy * w, dz * w
                else:
                    ax, ay, az = ax + dx * w, ay + dy * w, az + dz * w
            accel[t, 0] += ax
            accel[t, 1] += ay
            accel[t, 2] += az

    @pl.loop(0, own_blocks)
    def _(b):
        pull = jnp.sum(accel[b], axis=1)
        velocity_new = velocity_ref[b] + timestep * pull
        block = pool_ref[b]
        resident_ref[b, 0:3, :] = block[0:3] + timestep * velocity_new
        resident_ref[b, 3:4, :] = block[3:4]
        resident_ref[b, 4:7, :] = velocity_new

    outbox_ref[...] = jnp.zeros_like(outbox_ref)
    for g in range(used.shape[0]):
        used[g] = 0
    for m in range(departures_ref.shape[0]):
        d = departures_ref[m]
        owner = owners_ref[m]
        slot = used[owner]
        used[owner] = slot + 1
        outbox_ref[owner * slot_total + slot] = resident_ref[d]
        resident_ref[d] = jnp.zeros(resident_ref.shape[1:], jnp.float32)


def on_device(bodies, velocity, select, pair_target, pair_source, counts, departures, owners):
    own_blocks = bodies.shape[0]
    span = bodies.shape[2]
    pair_total = pair_target.shape[1]
    pool = bodies
    step = 0
    for axis in ("gx", "gy", "gz"):
        for bit in range(lax.axis_size(axis).bit_length() - 1):
            incoming = swapped(pool[select[0, step]], axis, bit)
            pool = jnp.concatenate([pool, incoming], axis=0)
            step += 1
    live = jnp.arange(pair_total, dtype=jnp.int32) < counts[0]
    targets = jnp.where(live, pair_target[0], own_blocks)
    sources = jnp.where(live, pair_source[0], 0)
    group_size = lax.axis_size("gz")
    move_count = departures.shape[1]
    slot_total = max(2, 2 * move_count // group_size)
    smem = pl.BlockSpec(memory_space=pltpu.SMEM)
    vmem = pl.BlockSpec(memory_space=pltpu.VMEM)
    resident, outbox = pl.pallas_call(
        functools.partial(step_kernel, slot_total),
        out_shape=(
            jax.ShapeDtypeStruct((own_blocks, 7, span), jnp.float32),
            jax.ShapeDtypeStruct((group_size * slot_total, 7, span), jnp.float32),
        ),
        in_specs=[smem] * 5 + [vmem] * 2,
        out_specs=(vmem, vmem),
        scratch_shapes=[
            pltpu.VMEM((pool.shape[0], span, 16), jnp.bfloat16),
            pltpu.VMEM((own_blocks + 1, 16, 4 * span), jnp.bfloat16),
            pltpu.VMEM((own_blocks + 1, 3, 8, span), jnp.float32),
            pltpu.SMEM((group_size,), jnp.int32),
        ],
        name="gravity",
    )(targets, sources, counts, departures[0], owners[:, 0], pool, velocity)
    arrived = lax.all_to_all(
        outbox.reshape(group_size, slot_total, 7, span), "gz", split_axis=0, concat_axis=0, tiled=True
    )
    return resident, arrived.reshape(group_size * slot_total, 7, span)


def solution(mesh):
    everywhere = ("gx", "gy", "gz")
    cube = P(everywhere, None, None)
    flat = P(everywhere, None)
    return jax.shard_map(
        on_device,
        mesh=mesh,
        in_specs=(cube, cube, cube, flat, flat, P(everywhere), flat, flat),
        out_specs=(cube, cube),
        check_vma=False,
    )
```

```python
import functools
import math

import jax
import jax.numpy as jnp
from jax import lax
from jax.experimental import pallas as pl
from jax.experimental.pallas import tpu as pltpu
from jax.sharding import PartitionSpec as P

soften = 0.01
timestep = 0.25
deepest_unroll = 32


def exchange_kernel(steps, select_ref, bodies_ref, pool_ref, outgoing, arriving, send_sem, recv_sem):
    own_blocks = bodies_ref.shape[0]
    send_count = outgoing.shape[1]
    partners = []
    for axis, stride in steps:
        me = lax.axis_index(axis)
        side = lax.rem(me // stride, 2)
        partners.append({axis: me + (1 - 2 * side) * stride})
    barrier = pltpu.get_barrier_semaphore()
    for partner in partners:
        pl.semaphore_signal(
            barrier, inc=1, device_id=partner, device_id_type=pl.DeviceIdType.MESH
        )
    pool_ref[0:own_blocks] = bodies_ref[...]
    pl.semaphore_wait(barrier, len(partners))
    copies = []
    for k, partner in enumerate(partners):
        for j in range(send_count):
            outgoing[k, j] = pool_ref[select_ref[k, j]]
        copy = pltpu.make_async_remote_copy(
            src_ref=outgoing.at[k],
            dst_ref=arriving.at[k],
            send_sem=send_sem.at[k],
            recv_sem=recv_sem.at[k],
            device_id=partner,
            device_id_type=pl.DeviceIdType.MESH,
        )
        copy.start()
        copies.append(copy)
        copy.wait_recv()
        base = own_blocks + k * send_count
        pool_ref[base : base + send_count] = arriving[k]
    for copy in copies:
        copy.wait_send()


def split(values):
    high = jnp.clip(values, -3.38e38, 3.38e38).astype(jnp.bfloat16).astype(jnp.float32)
    rest = values - high
    middle = rest.astype(jnp.bfloat16).astype(jnp.float32)
    return high, middle, rest - middle


def step_kernel(
    slot_total,
    target_ref,
    source_ref,
    count_ref,
    departures_ref,
    owners_ref,
    pool_ref,
    velocity_ref,
    resident_ref,
    outbox_ref,
    sources,
    targets,
    accel,
    used,
):
    pool_size = pool_ref.shape[0]
    own_blocks = velocity_ref.shape[0]
    span = pool_ref.shape[2]
    unroll = math.gcd(target_ref.shape[0], deepest_unroll)

    row = lax.broadcasted_iota(jnp.int32, (12, 4 * span), 0)
    lane = lax.broadcasted_iota(jnp.int32, (12, 4 * span), 1)
    picks = (row % 4 == lane // span).astype(jnp.float32)
    ones = (lax.broadcasted_iota(jnp.int32, (4, span), 0) < 3).astype(jnp.float32)

    batch = math.gcd(pool_size, 10)

    @pl.loop(0, pool_size // batch)
    def _(group):
        for b in [group * batch + u for u in range(batch)]:
            pieces = split(pool_ref[b])
            sources[b] = jnp.concatenate([*pieces, ones], axis=0).T.astype(jnp.bfloat16)

    @pl.loop(0, own_blocks + 1)
    def _(b):
        nothing = jnp.zeros((1, span), jnp.float32)
        rows = [
            jnp.concatenate([-piece[0:1], -piece[1:2], -piece[2:3], nothing], axis=1)
            for piece in split(pool_ref[b])
        ]
        rows.append(jnp.zeros((1, 4 * span), jnp.float32))
        targets[b] = jnp.concatenate([picks, *rows], axis=0).astype(jnp.bfloat16)

    accel[...] = jnp.zeros_like(accel)

    @pl.loop(0, (count_ref[0] + unroll - 1) // unroll)
    def _(group):
        for u in range(unroll):
            t = target_ref[group * unroll + u]
            s = source_ref[group * unroll + u]
            gaps = jnp.dot(sources[s], targets[t], preferred_element_type=jnp.float32)
            ax = ay = az = None
            for g in range(0, span, 8):
                dx = gaps[g : g + 8, 0:span]
                dy = gaps[g : g + 8, span : 2 * span]
                dz = gaps[g : g + 8, 2 * span : 3 * span]
                mass = gaps[g : g + 8, 3 * span :]
                inverse = lax.rsqrt(dx * dx + dy * dy + (dz * dz + soften))
                w = (mass * inverse) * (inverse * inverse)
                if ax is None:
                    ax, ay, az = dx * w, dy * w, dz * w
                else:
                    ax, ay, az = ax + dx * w, ay + dy * w, az + dz * w
            accel[t, 0] += ax
            accel[t, 1] += ay
            accel[t, 2] += az

    @pl.loop(0, own_blocks)
    def _(b):
        pull = jnp.sum(accel[b], axis=1)
        velocity_new = velocity_ref[b] + timestep * pull
        block = pool_ref[b]
        resident_ref[b, 0:3, :] = block[0:3] + timestep * velocity_new
        resident_ref[b, 3:4, :] = block[3:4]
        resident_ref[b, 4:7, :] = velocity_new

    outbox_ref[...] = jnp.zeros_like(outbox_ref)
    for g in range(used.shape[0]):
        used[g] = 0
    for m in range(departures_ref.shape[0]):
        d = departures_ref[m]
        owner = owners_ref[m]
        slot = used[owner]
        used[owner] = slot + 1
        outbox_ref[owner * slot_total + slot] = resident_ref[d]
        resident_ref[d] = jnp.zeros(resident_ref.shape[1:], jnp.float32)


def on_device(bodies, velocity, select, pair_target, pair_source, counts, departures, owners):
    own_blocks = bodies.shape[0]
    span = bodies.shape[2]
    pair_total = pair_target.shape[1]
    smem = pl.BlockSpec(memory_space=pltpu.SMEM)
    vmem = pl.BlockSpec(memory_space=pltpu.VMEM)
    steps = [
        (axis, 2**bit)
        for axis in ("gx", "gy", "gz")
        for bit in range(lax.axis_size(axis).bit_length() - 1)
    ]
    send_count = select.shape[2]
    slab = pltpu.VMEM((len(steps), send_count, 4, span), jnp.float32)
    pool = pl.pallas_call(
        functools.partial(exchange_kernel, steps),
        out_shape=jax.ShapeDtypeStruct((own_blocks + len(steps) * send_count, 4, span), jnp.float32),
        in_specs=[smem, vmem],
        out_specs=vmem,
        scratch_shapes=[
            slab,
            slab,
            pltpu.SemaphoreType.DMA((len(steps),)),
            pltpu.SemaphoreType.DMA((len(steps),)),
        ],
        compiler_params=pltpu.CompilerParams(collective_id=0, has_side_effects=True),
        name="exchange",
    )(select[0], bodies)
    live = jnp.arange(pair_total, dtype=jnp.int32) < counts[0]
    targets = jnp.where(live, pair_target[0], own_blocks)
    sources = jnp.where(live, pair_source[0], 0)
    group_size = lax.axis_size("gz")
    move_count = departures.shape[1]
    slot_total = max(2, 2 * move_count // group_size)
    resident, outbox = pl.pallas_call(
        functools.partial(step_kernel, slot_total),
        out_shape=(
            jax.ShapeDtypeStruct((own_blocks, 7, span), jnp.float32),
            jax.ShapeDtypeStruct((group_size * slot_total, 7, span), jnp.float32),
        ),
        in_specs=[smem] * 5 + [vmem] * 2,
        out_specs=(vmem, vmem),
        scratch_shapes=[
            pltpu.VMEM((pool.shape[0], span, 16), jnp.bfloat16),
            pltpu.VMEM((own_blocks + 1, 16, 4 * span), jnp.bfloat16),
            pltpu.VMEM((own_blocks + 1, 3, 8, span), jnp.float32),
            pltpu.SMEM((group_size,), jnp.int32),
        ],
        name="gravity",
    )(targets, sources, counts, departures[0], owners[:, 0], pool, velocity)
    arrived = lax.all_to_all(
        outbox.reshape(group_size, slot_total, 7, span), "gz", split_axis=0, concat_axis=0, tiled=True
    )
    return resident, arrived.reshape(group_size * slot_total, 7, span)


def solution(mesh):
    everywhere = ("gx", "gy", "gz")
    cube = P(everywhere, None, None)
    flat = P(everywhere, None)
    return jax.shard_map(
        on_device,
        mesh=mesh,
        in_specs=(cube, cube, cube, flat, flat, P(everywhere), flat, flat),
        out_specs=(cube, cube),
        check_vma=False,
    )
```

```python
import functools
import math

import jax
import jax.numpy as jnp
from jax import lax
from jax.experimental import pallas as pl
from jax.experimental.pallas import tpu as pltpu
from jax.sharding import PartitionSpec as P

soften = 0.01
timestep = 0.25
deepest_unroll = 32


def exchange_kernel(steps, select_ref, bodies_ref, pool_ref, outgoing, arriving, send_sem, recv_sem):
    own_blocks = bodies_ref.shape[0]
    send_count = outgoing.shape[1]
    partners = []
    for axis, stride in steps:
        me = lax.axis_index(axis)
        side = lax.rem(me // stride, 2)
        partners.append({axis: me + (1 - 2 * side) * stride})
    barrier = pltpu.get_barrier_semaphore()
    for partner in partners:
        pl.semaphore_signal(
            barrier, inc=1, device_id=partner, device_id_type=pl.DeviceIdType.MESH
        )
    pool_ref[0:own_blocks] = bodies_ref[...]
    pl.semaphore_wait(barrier, len(partners))
    copies = []
    for k, partner in enumerate(partners):
        for j in range(send_count):
            outgoing[k, j] = pool_ref[select_ref[k, 0, j]]
        copy = pltpu.make_async_remote_copy(
            src_ref=outgoing.at[k],
            dst_ref=arriving.at[k],
            send_sem=send_sem.at[k],
            recv_sem=recv_sem.at[k],
            device_id=partner,
            device_id_type=pl.DeviceIdType.MESH,
        )
        copy.start()
        copies.append(copy)
        copy.wait_recv()
        base = own_blocks + k * send_count
        pool_ref[base : base + send_count] = arriving[k]
    for copy in copies:
        copy.wait_send()


def split(values):
    high = jnp.clip(values, -3.38e38, 3.38e38).astype(jnp.bfloat16).astype(jnp.float32)
    rest = values - high
    middle = rest.astype(jnp.bfloat16).astype(jnp.float32)
    return high, middle, rest - middle


def step_kernel(
    slot_total,
    target_ref,
    source_ref,
    count_ref,
    departures_ref,
    owners_ref,
    pool_ref,
    velocity_ref,
    resident_ref,
    outbox_ref,
    sources,
    targets,
    accel,
    used,
):
    pool_size = pool_ref.shape[0]
    own_blocks = velocity_ref.shape[1]
    span = pool_ref.shape[2]
    unroll = math.gcd(target_ref.shape[0], deepest_unroll)

    row = lax.broadcasted_iota(jnp.int32, (12, 4 * span), 0)
    lane = lax.broadcasted_iota(jnp.int32, (12, 4 * span), 1)
    picks = (row % 4 == lane // span).astype(jnp.float32)
    ones = (lax.broadcasted_iota(jnp.int32, (4, span), 0) < 3).astype(jnp.float32)

    batch = math.gcd(pool_size, 10)

    @pl.loop(0, pool_size // batch)
    def _(group):
        for b in [group * batch + u for u in range(batch)]:
            pieces = split(pool_ref[b])
            sources[b] = jnp.concatenate([*pieces, ones], axis=0).T.astype(jnp.bfloat16)

    own_batch = math.gcd(own_blocks, 12)

    @pl.loop(0, own_blocks // own_batch)
    def _(group):
        for b in [group * own_batch + u for u in range(own_batch)]:
            nothing = jnp.zeros((1, span), jnp.float32)
            rows = [
                jnp.concatenate([-piece[0:1], -piece[1:2], -piece[2:3], nothing], axis=1)
                for piece in split(pool_ref[b])
            ]
            rows.append(jnp.zeros((1, 4 * span), jnp.float32))
            targets[b] = jnp.concatenate([picks, *rows], axis=0).astype(jnp.bfloat16)

    targets[own_blocks] = jnp.zeros(targets.shape[1:], jnp.bfloat16)
    accel[...] = jnp.zeros_like(accel)

    @pl.loop(0, (count_ref[0] + unroll - 1) // unroll)
    def _(group):
        for u in range(unroll):
            t = jnp.where(group * unroll + u < count_ref[0], target_ref[group * unroll + u], own_blocks)
            s = source_ref[group * unroll + u]
            gaps = jnp.dot(sources[s], targets[t], preferred_element_type=jnp.float32)
            ax = ay = az = None
            for g in range(0, span, 8):
                dx = gaps[g : g + 8, 0:span]
                dy = gaps[g : g + 8, span : 2 * span]
                dz = gaps[g : g + 8, 2 * span : 3 * span]
                mass = gaps[g : g + 8, 3 * span :]
                inverse = lax.rsqrt(dx * dx + dy * dy + (dz * dz + soften))
                w = (mass * inverse) * (inverse * inverse)
                if ax is None:
                    ax, ay, az = dx * w, dy * w, dz * w
                else:
                    ax, ay, az = ax + dx * w, ay + dy * w, az + dz * w
            accel[t, 0] += ax
            accel[t, 1] += ay
            accel[t, 2] += az

    @pl.loop(0, own_blocks // own_batch)
    def _(group):
        for b in [group * own_batch + u for u in range(own_batch)]:
            row = pl.ds(b, 1)
            for c in range(3):
                pull = jnp.sum(accel[b, c], axis=0, keepdims=True)
                velocity_new = velocity_ref[c, row, :] + timestep * pull
                resident_ref[c, row, :] = pool_ref[b, c : c + 1, :] + timestep * velocity_new
                resident_ref[4 + c, row, :] = velocity_new
            resident_ref[3, row, :] = pool_ref[b, 3:4, :]

    outbox_ref[...] = jnp.zeros_like(outbox_ref)
    for g in range(used.shape[0]):
        used[g] = 0
    for m in range(departures_ref.shape[0]):
        d = departures_ref[m]
        owner = owners_ref[m]
        slot = used[owner]
        used[owner] = slot + 1
        for c in range(resident_ref.shape[0]):
            outbox_ref[owner * slot_total + slot, c : c + 1, :] = resident_ref[c, pl.ds(d, 1), :]
            resident_ref[c, pl.ds(d, 1), :] = jnp.zeros((1, span), jnp.float32)


def on_device(bodies, velocity, select, pair_target, pair_source, counts, departures, owners):
    own_blocks = bodies.shape[0]
    span = bodies.shape[2]
    smem = pl.BlockSpec(memory_space=pltpu.SMEM)
    vmem = pl.BlockSpec(memory_space=pltpu.VMEM)
    steps = [
        (axis, 2**bit)
        for axis in ("gx", "gy", "gz")
        for bit in range(lax.axis_size(axis).bit_length() - 1)
    ]
    send_count = select.shape[2]
    slab = pltpu.VMEM((len(steps), send_count, 4, span), jnp.float32)
    pool = pl.pallas_call(
        functools.partial(exchange_kernel, steps),
        out_shape=jax.ShapeDtypeStruct((own_blocks + len(steps) * send_count, 4, span), jnp.float32),
        in_specs=[smem, vmem],
        out_specs=vmem,
        scratch_shapes=[
            slab,
            slab,
            pltpu.SemaphoreType.DMA((len(steps),)),
            pltpu.SemaphoreType.DMA((len(steps),)),
        ],
        compiler_params=pltpu.CompilerParams(collective_id=0, has_side_effects=True),
        name="exchange",
    )(jnp.transpose(select, (1, 0, 2)), bodies)
    group_size = lax.axis_size("gz")
    move_count = departures.shape[1]
    slot_total = max(2, 2 * move_count // group_size)
    resident, outbox = pl.pallas_call(
        functools.partial(step_kernel, slot_total),
        out_shape=(
            jax.ShapeDtypeStruct((7, own_blocks, span), jnp.float32),
            jax.ShapeDtypeStruct((group_size * slot_total, 7, span), jnp.float32),
        ),
        in_specs=[smem] * 5 + [vmem] * 2,
        out_specs=(vmem, vmem),
        scratch_shapes=[
            pltpu.VMEM((pool.shape[0], span, 16), jnp.bfloat16),
            pltpu.VMEM((own_blocks + 1, 16, 4 * span), jnp.bfloat16),
            pltpu.VMEM((own_blocks + 1, 3, 8, span), jnp.float32),
            pltpu.SMEM((group_size,), jnp.int32),
        ],
        name="gravity",
    )(
        pair_target[0],
        pair_source[0],
        counts,
        departures[0],
        owners[:, 0],
        pool,
        jnp.transpose(velocity, (1, 0, 2)),
    )
    arrived = lax.all_to_all(
        outbox.reshape(group_size, slot_total, 7, span), "gz", split_axis=0, concat_axis=0, tiled=True
    )
    return jnp.transpose(resident, (1, 0, 2)), arrived.reshape(group_size * slot_total, 7, span)


def solution(mesh):
    everywhere = ("gx", "gy", "gz")
    cube = P(everywhere, None, None)
    flat = P(everywhere, None)
    return jax.shard_map(
        on_device,
        mesh=mesh,
        in_specs=(cube, cube, cube, flat, flat, P(everywhere), flat, flat),
        out_specs=(cube, cube),
        check_vma=False,
    )
```

```python
import functools
import math

import jax
import jax.numpy as jnp
from jax import lax
from jax.experimental import pallas as pl
from jax.experimental.pallas import tpu as pltpu
from jax.sharding import PartitionSpec as P

soften = 0.01
timestep = 0.25
deepest_unroll = 64


def exchange_kernel(steps, select_ref, bodies_ref, pool_ref, outgoing, arriving, send_sem, recv_sem):
    own_blocks = bodies_ref.shape[0]
    send_count = outgoing.shape[1]
    partners = []
    for axis, stride in steps:
        me = lax.axis_index(axis)
        side = lax.rem(me // stride, 2)
        partners.append({axis: me + (1 - 2 * side) * stride})
    barrier = pltpu.get_barrier_semaphore()
    for partner in partners:
        pl.semaphore_signal(
            barrier, inc=1, device_id=partner, device_id_type=pl.DeviceIdType.MESH
        )
    pool_ref[0:own_blocks] = bodies_ref[...]
    pl.semaphore_wait(barrier, len(partners))
    copies = []
    for k, partner in enumerate(partners):
        for j in range(send_count):
            outgoing[k, j] = pool_ref[select_ref[k, 0, j]]
        copy = pltpu.make_async_remote_copy(
            src_ref=outgoing.at[k],
            dst_ref=arriving.at[k],
            send_sem=send_sem.at[k],
            recv_sem=recv_sem.at[k],
            device_id=partner,
            device_id_type=pl.DeviceIdType.MESH,
        )
        copy.start()
        copies.append(copy)
        copy.wait_recv()
        base = own_blocks + k * send_count
        pool_ref[base : base + send_count] = arriving[k]
    for copy in copies:
        copy.wait_send()


def split(values):
    high = jnp.clip(values, -3.38e38, 3.38e38).astype(jnp.bfloat16).astype(jnp.float32)
    rest = values - high
    middle = rest.astype(jnp.bfloat16).astype(jnp.float32)
    return high, middle, rest - middle


def step_kernel(
    slot_total,
    target_ref,
    source_ref,
    count_ref,
    departures_ref,
    owners_ref,
    pool_ref,
    velocity_ref,
    resident_ref,
    outbox_ref,
    sources,
    targets,
    accel,
    used,
):
    pool_size = pool_ref.shape[0]
    own_blocks = velocity_ref.shape[1]
    span = pool_ref.shape[2]
    unroll = math.gcd(target_ref.shape[0], deepest_unroll)

    row = lax.broadcasted_iota(jnp.int32, (12, 4 * span), 0)
    lane = lax.broadcasted_iota(jnp.int32, (12, 4 * span), 1)
    picks = (row % 4 == lane // span).astype(jnp.float32)
    ones = (lax.broadcasted_iota(jnp.int32, (4, span), 0) < 3).astype(jnp.float32)

    batch = math.gcd(pool_size, 10)

    @pl.loop(0, pool_size // batch)
    def _(group):
        for b in [group * batch + u for u in range(batch)]:
            pieces = split(pool_ref[b])
            sources[b] = jnp.concatenate([*pieces, ones], axis=0).T.astype(jnp.bfloat16)

    own_batch = math.gcd(own_blocks, 12)

    @pl.loop(0, own_blocks // own_batch)
    def _(group):
        for b in [group * own_batch + u for u in range(own_batch)]:
            nothing = jnp.zeros((1, span), jnp.float32)
            rows = [
                jnp.concatenate([-piece[0:1], -piece[1:2], -piece[2:3], nothing], axis=1)
                for piece in split(pool_ref[b])
            ]
            rows.append(jnp.zeros((1, 4 * span), jnp.float32))
            targets[b] = jnp.concatenate([picks, *rows], axis=0).astype(jnp.bfloat16)

    targets[own_blocks] = jnp.zeros(targets.shape[1:], jnp.bfloat16)
    accel[...] = jnp.zeros_like(accel)

    @pl.loop(0, (count_ref[0] + unroll - 1) // unroll)
    def _(group):
        for u in range(unroll):
            t = jnp.where(group * unroll + u < count_ref[0], target_ref[group * unroll + u], own_blocks)
            s = source_ref[group * unroll + u]
            gaps = jnp.dot(sources[s], targets[t], preferred_element_type=jnp.float32)
            ax = ay = az = None
            for g in range(0, span, 8):
                dx = gaps[g : g + 8, 0:span]
                dy = gaps[g : g + 8, span : 2 * span]
                dz = gaps[g : g + 8, 2 * span : 3 * span]
                mass = gaps[g : g + 8, 3 * span :]
                inverse = lax.rsqrt(dx * dx + dy * dy + (dz * dz + soften))
                w = (mass * inverse) * (inverse * inverse)
                if ax is None:
                    ax, ay, az = dx * w, dy * w, dz * w
                else:
                    ax, ay, az = ax + dx * w, ay + dy * w, az + dz * w
            accel[t, 0] += ax
            accel[t, 1] += ay
            accel[t, 2] += az

    @pl.loop(0, own_blocks // own_batch)
    def _(group):
        for b in [group * own_batch + u for u in range(own_batch)]:
            row = pl.ds(b, 1)
            for c in range(3):
                pull = jnp.sum(accel[b, c], axis=0, keepdims=True)
                velocity_new = velocity_ref[c, row, :] + timestep * pull
                resident_ref[c, row, :] = pool_ref[b, c : c + 1, :] + timestep * velocity_new
                resident_ref[4 + c, row, :] = velocity_new
            resident_ref[3, row, :] = pool_ref[b, 3:4, :]

    outbox_ref[...] = jnp.zeros_like(outbox_ref)
    for g in range(used.shape[0]):
        used[g] = 0
    for m in range(departures_ref.shape[0]):
        d = departures_ref[m]
        owner = owners_ref[m]
        slot = used[owner]
        used[owner] = slot + 1
        for c in range(resident_ref.shape[0]):
            outbox_ref[owner * slot_total + slot, c : c + 1, :] = resident_ref[c, pl.ds(d, 1), :]
            resident_ref[c, pl.ds(d, 1), :] = jnp.zeros((1, span), jnp.float32)


def on_device(bodies, velocity, select, pair_target, pair_source, counts, departures, owners):
    own_blocks = bodies.shape[0]
    span = bodies.shape[2]
    smem = pl.BlockSpec(memory_space=pltpu.SMEM)
    vmem = pl.BlockSpec(memory_space=pltpu.VMEM)
    steps = [
        (axis, 2**bit)
        for axis in ("gx", "gy", "gz")
        for bit in range(lax.axis_size(axis).bit_length() - 1)
    ]
    send_count = select.shape[2]
    slab = pltpu.VMEM((len(steps), send_count, 4, span), jnp.float32)
    pool = pl.pallas_call(
        functools.partial(exchange_kernel, steps),
        out_shape=jax.ShapeDtypeStruct((own_blocks + len(steps) * send_count, 4, span), jnp.float32),
        in_specs=[smem, vmem],
        out_specs=vmem,
        scratch_shapes=[
            slab,
            slab,
            pltpu.SemaphoreType.DMA((len(steps),)),
            pltpu.SemaphoreType.DMA((len(steps),)),
        ],
        compiler_params=pltpu.CompilerParams(collective_id=0, has_side_effects=True),
        name="exchange",
    )(jnp.transpose(select, (1, 0, 2)), bodies)
    group_size = lax.axis_size("gz")
    move_count = departures.shape[1]
    slot_total = max(2, 2 * move_count // group_size)
    resident, outbox = pl.pallas_call(
        functools.partial(step_kernel, slot_total),
        out_shape=(
            jax.ShapeDtypeStruct((7, own_blocks, span), jnp.float32),
            jax.ShapeDtypeStruct((group_size * slot_total, 7, span), jnp.float32),
        ),
        in_specs=[smem] * 5 + [vmem] * 2,
        out_specs=(vmem, vmem),
        scratch_shapes=[
            pltpu.VMEM((pool.shape[0], span, 16), jnp.bfloat16),
            pltpu.VMEM((own_blocks + 1, 16, 4 * span), jnp.bfloat16),
            pltpu.VMEM((own_blocks + 1, 3, 8, span), jnp.float32),
            pltpu.SMEM((group_size,), jnp.int32),
        ],
        name="gravity",
    )(
        pair_target[0],
        pair_source[0],
        counts,
        departures[0],
        owners[:, 0],
        pool,
        jnp.transpose(velocity, (1, 0, 2)),
    )
    arrived = lax.all_to_all(
        outbox.reshape(group_size, slot_total, 7, span), "gz", split_axis=0, concat_axis=0, tiled=True
    )
    return jnp.transpose(resident, (1, 0, 2)), arrived.reshape(group_size * slot_total, 7, span)


def solution(mesh):
    everywhere = ("gx", "gy", "gz")
    cube = P(everywhere, None, None)
    flat = P(everywhere, None)
    return jax.shard_map(
        on_device,
        mesh=mesh,
        in_specs=(cube, cube, cube, flat, flat, P(everywhere), flat, flat),
        out_specs=(cube, cube),
        check_vma=False,
    )
```
